32 devices in a mesh: tp: 2 (over x), rows: 16 (over z, y, core).
Axes of the slice: x: 2, y: 2, z: 4, core: 2. Of those that a mesh axis runs over, the one named last changes fastest.
Arguments:
- patches: bfloat16 [16, 2048, 1152], P('rows', 'tp'), may hold values from -6 to 6
- image_lengths: int32 [16, 4], P('rows'), may hold values from 256 to 1024, as said below
- ln_gain: float32 [2, 1152], replicated, may hold values from 0.5 to 1.5
- ln_bias: float32 [2, 1152], replicated, may hold values from -4 to 4
- query_key_value_weight: bfloat16 [3, 1152, 1152], P(None, 'rows', 'tp'), may hold values from -0.1875 to 0.1875
- out_weight: bfloat16 [1152, 1152], P('rows', 'tp'), may hold values from -1.5 to 1.5
- up_weight: bfloat16 [1152, 4304], P('rows', 'tp'), may hold values from -0.1875 to 0.1875
- down_weight: bfloat16 [1152, 4304], P('rows', 'tp'), may hold values from -0.09375 to 0.09375
- adapter: float32 [2, 55296], P(None, ('tp', 'rows')), may hold values from -0.1875 to 0.1875
- adapter_mean: float32 [2, 55296], P(None, ('tp', 'rows')), may hold values from -3 to 3
- adapter_square: float32 [2, 55296], P(None, ('tp', 'rows')), may hold values from 0.01 to 1
- cotangent: bfloat16 [16, 2048, 1152], P('rows', 'tp'), may hold values from -6 to 6
Outputs:
- output: bfloat16 [16, 2048, 1152], P('rows', 'tp')
- patch_grad: float32 [16, 2048, 1152], P('rows', 'tp')
- adapter_grad: float32 [2, 55296], P(None, ('tp', 'rows'))
- new_adapter: float32 [2, 55296], P(None, ('tp', 'rows'))
- new_mean: float32 [2, 55296], P(None, ('tp', 'rows'))
- new_square: float32 [2, 55296], P(None, ('tp', 'rows'))
The draws below stay inside these ranges and needn't reach their ends.
Inputs may be any that keep to these rules, and one draw needn't show every extreme that they name: `image_lengths`: each pack holds 4 images laid end to end whose patch counts sum to 2048; in every pack one image has exactly 1024 patches and some image has exactly 256.
All inputs are finite; a program needn't handle non-finite values.
Results may differ from the reference program's by a relative error of at most 0.013.
Values may be sent and summed in bfloat16 or wider, within the bound.
No kernel may reach another device: no remote copies, remote signals or barrier semaphores. Data moves between devices by JAX's collectives and lax.ppermute only.
A program may use at most 256 MiB of HBM per device.

```python
import math
import jax
import jax.numpy as jnp
from jax import lax

D = 1152
HEADS = 16
HD = 72
FF = 4304
RANK = 16
IMGS = 4
PACK = 2048
MIN_IMG = 256
PACKS = 16
TOKENS = 32768


def draw_image_lengths(key, part):
    key_weights = jax.random.fold_in(key, 11)
    key_zero = jax.random.fold_in(key, 12)
    key_place = jax.random.fold_in(key, 13)
    others = IMGS - 1
    weights = jax.random.randint(key_weights, (PACKS, others), 1, 101, dtype=jnp.int32)
    zero_at = jax.random.randint(key_zero, (PACKS, 1), 0, others, dtype=jnp.int32)
    slot_index = jnp.arange(others, dtype=jnp.int32)[None, :]
    weights = jnp.where(slot_index == zero_at, 0, weights).astype(jnp.int32)
    spare = PACK // 2 - others * MIN_IMG
    total = jnp.sum(weights, axis=1, keepdims=True).astype(jnp.int32)
    share = spare * weights // total
    leftover = spare - jnp.sum(share, axis=1, keepdims=True)
    give_at = (zero_at + 1) % others
    share = share + jnp.where(slot_index == give_at, leftover, 0)
    other_lengths = (MIN_IMG + share).astype(jnp.int32)
    place = jax.random.randint(key_place, (PACKS, 1), 0, IMGS, dtype=jnp.int32)
    slots = jnp.arange(IMGS, dtype=jnp.int32)[None, :]
    below = jnp.take_along_axis(other_lengths, jnp.broadcast_to(jnp.minimum(slots, others - 1), (PACKS, IMGS)), axis=1)
    above = jnp.take_along_axis(other_lengths, jnp.broadcast_to(jnp.maximum(slots - 1, 0), (PACKS, IMGS)), axis=1)
    result = jnp.where(slots < place, below, jnp.where(slots == place, PACK // 2, above))
    return result.astype(jnp.int32)


def levels(key, extent, split, least, top_value):
    factor_of, own = 1.0, jax.random.fold_in(key, 6)
    for position, parts in split:
        heights = jnp.exp(jax.random.uniform(jax.random.fold_in(own, position), (parts,), jnp.float32, least / len(split), top_value / len(split)))
        factor_of = factor_of * jnp.repeat(heights, extent[position] // parts).reshape([-1 if axis == position else 1 for axis in range(len(extent))])
    return factor_of


def gaussian(stream_key, dims, scale, reach, shards=(), kind=jnp.bfloat16):
    loudness = levels(stream_key, dims, shards, -0.22, 0.18) if shards else 1.0
    drawn = jax.random.normal(stream_key, dims, jnp.float32) * scale * loudness
    return jnp.minimum(jnp.maximum(drawn, -reach), reach).astype(kind)


def setup_inputs(seed: int = 0) -> dict:
    key_list = jax.random.split(jax.random.key(seed), 13)
    return {
        "patches": gaussian(key_list[0], (PACKS, PACK, D), 1.0, 6.0, ((0, 16), (1, 2))),
        "image_lengths": draw_image_lengths(jax.random.fold_in(key_list[12], 71), 0),
        "ln_gain": jnp.clip(1.0 + 0.1 * jax.random.normal(key_list[2], (2, D), jnp.float32), 0.5, 1.5),
        "ln_bias": gaussian(key_list[3], (2, D), 0.3, 4.0, (), jnp.float32),
        "query_key_value_weight": gaussian(key_list[4], (3, D, HEADS * HD), D ** -0.5, 0.1875, ((1, 16), (2, 2))),
        "out_weight": gaussian(key_list[5], (D, HEADS * HD), (D // 64) ** -0.5, 1.5, ((0, 16), (1, 2))),
        "up_weight": gaussian(key_list[6], (D, FF), D ** -0.5, 0.1875, ((0, 16), (1, 2))),
        "down_weight": gaussian(key_list[7], (D, FF), FF ** -0.5, 0.09375, ((0, 16), (1, 2))),
        "adapter": gaussian(key_list[8], (2, 3 * D * RANK), D ** -0.5, 0.1875, ((1, 32),), jnp.float32),
        "adapter_mean": gaussian(key_list[9], (2, 3 * D * RANK), 0.3, 3.0, ((1, 32),), jnp.float32),
        "adapter_square": jnp.clip(jnp.exp(math.log(1.0) - 4.6051702 * jax.random.uniform(key_list[10], (2, 3 * D * RANK), jnp.float32) ** levels(key_list[10], (2, 3 * D * RANK), ((1, 32),), -0.2, 0.2)), 0.01, 1.0),
        "cotangent": gaussian(key_list[11], (PACKS, PACK, D), 1.0, 6.0, ((0, 16), (1, 2))),
    }


@jax.custom_vjp
def low(v):
    return lax.optimization_barrier(v.astype(jnp.bfloat16)).astype(jnp.float32)

@jax.custom_vjp
def low_back(v):
    return v

def low_keep(v):
    return (low(v), None)

def low_pass(kept, grad):
    return (grad,)

def back_keep(v):
    return (v, None)

def back_low(kept, grad):
    return (low(grad),)
low.defvjp(low_keep, low_pass)
low_back.defvjp(back_keep, back_low)
ln_eps = 1e-06
adapter_scale = 2.0
beta_one = 0.9
beta_two = 0.999
adam_eps = 1e-08
learn_rate = 0.01
decay_rate = 0.01
adam_step = 10.0
gelu_coeff = 0.7978845608028654

def matrix_product(left, right):
    return jnp.dot(left, right, precision=lax.Precision.HIGHEST, preferred_element_type=jnp.float32)

def layer_norm(values, gain, shift):
    center = lax.optimization_barrier(jnp.mean(values, axis=-1, keepdims=True))
    centred = values - center
    spread = lax.optimization_barrier(jnp.mean(centred * centred, axis=-1, keepdims=True))
    return centred * lax.rsqrt(spread + ln_eps) * gain + shift

def gelu_tanh(value):
    return 0.5 * value * (1.0 + jnp.tanh(gelu_coeff * (value + 0.044715 * value * value * value)))

def attend(query, keys, values, segment):
    block = min(512, PACK)
    blocks = PACK // block
    query_heads = query.reshape(blocks, block, HEADS, HD)
    key_heads = keys.reshape(PACK, HEADS, HD)
    value_heads = values.reshape(PACK, HEADS, HD)

    @jax.checkpoint
    def one_block(inputs):
        query_block, segment_block = inputs
        scores = jnp.einsum('qhd,khd->hqk', query_block, key_heads, precision=lax.Precision.HIGHEST) * HD ** (-0.5)
        scores = low_back(scores)
        same_image = segment_block[:, None] == segment[None, :]
        scores = jnp.where(same_image[None], scores, -jnp.inf)
        highest = lax.optimization_barrier(jnp.max(scores, axis=-1, keepdims=True))
        weights = jnp.exp(scores - highest)
        probs = weights / lax.optimization_barrier(jnp.sum(weights, axis=-1, keepdims=True))
        return jnp.einsum('hqk,khd->qhd', low(probs), value_heads, precision=lax.Precision.HIGHEST)
    mixed = lax.map(one_block, (query_heads, segment.reshape(blocks, block)))
    return mixed.reshape(PACK, HEADS * HD)

def forward(values, adapter, segment, ln_gain, ln_bias, query_key_value_weight, out_weight, up_weight, down_weight):
    first_normed = low(layer_norm(values, ln_gain[0], ln_bias[0]))
    downs = low(adapter[0].reshape(3, D, RANK))
    up_adapters = low(adapter[1].reshape(3, D, RANK))
    projected = []
    for slot_index in range(3):
        inner_product = low(matrix_product(first_normed, downs[slot_index]))
        complete_rows = matrix_product(first_normed, query_key_value_weight[slot_index]) + adapter_scale * matrix_product(inner_product, up_adapters[slot_index].T)
        projected.append(low_back(low(complete_rows)))
    attended = low_back(low(attend(projected[0], projected[1], projected[2], segment)))
    mixed = values + low_back(matrix_product(attended, out_weight.T))
    normed_two = low(layer_norm(mixed, ln_gain[1], ln_bias[1]))
    hidden = low_back(matrix_product(normed_two, up_weight))
    active = low(gelu_tanh(hidden))
    return mixed + low_back(matrix_product(active, down_weight.T))

def reference(patches, image_lengths, ln_gain, ln_bias, query_key_value_weight, out_weight, up_weight, down_weight, adapter, adapter_mean, adapter_square, cotangent):
    qkv_full = query_key_value_weight.astype(jnp.float32)
    out_full = out_weight.astype(jnp.float32)
    up_full = up_weight.astype(jnp.float32)
    down_full = down_weight.astype(jnp.float32)
    positions = jnp.arange(PACK, dtype=jnp.int32)

    def one_pack(summed_total, item):
        values, lengths, upstream = item
        ends = jnp.cumsum(lengths, dtype=jnp.int32)
        segment = lax.optimization_barrier(jnp.sum((positions[:, None] >= ends[None, :]).astype(jnp.int32), axis=1)).astype(jnp.int32)

        def local(values_in, adapter_in):
            return forward(values_in, adapter_in, segment, ln_gain, ln_bias, qkv_full, out_full, up_full, down_full)
        result, pullback = jax.vjp(local, values.astype(jnp.float32), adapter)
        d_values, d_adapter = pullback(upstream.astype(jnp.float32))
        return (summed_total + d_adapter, (result.astype(jnp.bfloat16), d_values))
    summed_total, (output, patch_grad) = lax.scan(one_pack, jnp.zeros_like(adapter), (patches, image_lengths, cotangent))
    adapter_grad = summed_total / math.sqrt(TOKENS)
    new_mean = beta_one * adapter_mean + (1.0 - beta_one) * adapter_grad
    new_square = beta_two * adapter_square + (1.0 - beta_two) * adapter_grad * adapter_grad
    fixed_mean = new_mean / (1.0 - beta_one ** adam_step)
    fixed_square = new_square / (1.0 - beta_two ** adam_step)
    new_adapter = adapter - learn_rate * (fixed_mean / (jnp.sqrt(fixed_square) + adam_eps) + decay_rate * adapter)
    return (output, patch_grad, adapter_grad, new_adapter, new_mean, new_square)
```

```python
import functools
import math

import jax
import jax.numpy as jnp
from jax import lax
from jax.experimental import pallas as pl
from jax.experimental.pallas import tpu as pltpu
from jax.sharding import PartitionSpec as P

HD = 72
RANK = 16
LANES = 128

ln_eps = 1e-06
adapter_scale = 2.0
beta_one = 0.9
beta_two = 0.999
adam_eps = 1e-08
learn_rate = 0.01
decay_rate = 0.01
adam_step = 10.0
gelu_coeff = 0.7978845608028654
log2_e = 1.4426950408889634
score_scale = HD ** (-0.5)

f32 = jnp.float32
bf16 = jnp.bfloat16
VMEM_LIMIT = 60 * 2**20


def dot(left, right, left_dim, right_dim):
    return lax.dot_general(
        left, right, (((left_dim,), (right_dim,)), ((), ())), preferred_element_type=f32
    )


def call(kernel, grid, in_specs, out_specs, out_shape, scratch=()):
    return pl.pallas_call(
        kernel,
        grid=grid,
        in_specs=in_specs,
        out_specs=out_specs,
        out_shape=out_shape,
        scratch_shapes=list(scratch),
        compiler_params=pltpu.CompilerParams(vmem_limit_bytes=VMEM_LIMIT),
    )


def whole(shape):
    return pl.BlockSpec(shape, lambda *_: (0,) * len(shape))


def struct(shape, dtype):
    return jax.ShapeDtypeStruct(shape, dtype)


def lane_loop(count, body):
    def step(i, carry):
        body(pl.ds(pl.multiple_of(i * LANES, LANES), LANES))
        return carry

    lax.fori_loop(0, count // LANES, step, 0)


def project_kernel(qkv_width, x_ref, gain_ref, shift_ref, downs_ref, ups_ref, w_ref,
                   qkv_ref, xt_ref, normed_ref, inner_ref):
    length = x_ref.shape[0]

    @pl.when(pl.program_id(0) == 0)
    def _():
        def norm(at):
            v = x_ref[at, :].astype(f32).T
            xt_ref[:, at] = v.astype(bf16)
            centred = v - jnp.mean(v, axis=0, keepdims=True)
            inverse = lax.rsqrt(jnp.mean(centred * centred, axis=0, keepdims=True) + ln_eps)
            normed_ref[:, at] = (centred * inverse * gain_ref[...] + shift_ref[...]).astype(bf16)

        lane_loop(length, norm)
        inner_ref[...] = dot(downs_ref[...], normed_ref[...], 1, 0).astype(bf16)

    width = qkv_width // 3
    acc = dot(w_ref[:, :qkv_width], normed_ref[...], 0, 0)
    acc = acc + adapter_scale * dot(ups_ref[...], inner_ref[...], 0, 0)
    qkv_ref[:width, :] = (acc[:width] * (score_scale * log2_e)).astype(bf16)
    qkv_ref[width:, :] = acc[width:].astype(bf16)


def attend_kernel(q_ref, k_ref, v_ref, seg_col_ref, seg_row_ref, out_ref, probs_ref, inv_ref):
    length = q_ref.shape[1]
    scores = dot(k_ref[...], q_ref[...], 0, 0)
    seg_col = jnp.concatenate([seg_col_ref[...]] * (length // LANES), axis=1)
    scores = jnp.where(seg_col == seg_row_ref[...], scores, -1e30)
    highest = jnp.max(scores, axis=0, keepdims=True)
    weights = jnp.exp2(scores - highest)
    inverse = 1.0 / jnp.sum(weights, axis=0, keepdims=True)
    probs = weights.astype(bf16)
    probs_ref[...] = probs
    inv_ref[...] = inverse
    out_ref[...] = (dot(v_ref[...], probs, 1, 0) * inverse).astype(bf16)


def attend_back_kernel(probs_ref, inv_ref, q_ref, k_ref, v_ref, grad_ref, out_ref,
                       dqkv_ref):
    grad = grad_ref[...].astype(f32) * inv_ref[...]
    delta = jnp.sum(grad * out_ref[...].astype(f32), axis=0, keepdims=True)
    grad = grad.astype(bf16)
    probs = probs_ref[...]
    d_probs = dot(v_ref[...], grad, 0, 0)
    d_scores = (probs.astype(f32) * (d_probs - delta)).astype(bf16)
    dqkv_ref[0] = (dot(k_ref[...], d_scores, 1, 0) * score_scale).astype(bf16)
    dqkv_ref[1] = (dot(q_ref[...], d_scores, 1, 1) * (1.0 / log2_e)).astype(bf16)
    dqkv_ref[2] = dot(grad, probs, 1, 1).astype(bf16)


def mix_kernel(skip, xt_ref, att_ref, w_ref, gain_ref, shift_ref, cot_ref,
               mixed_ref, normed_ref, cot_t_ref, w_buf, padded, sem):
    length = xt_ref.shape[1]
    copies = []
    for t in range(2):
        copies.append(pltpu.make_async_copy(w_ref.at[t, :, pl.ds(w_ref.shape[2] - w_buf.shape[2], w_buf.shape[2])],
                                            w_buf.at[t], sem.at[t]))
        copies[t].start()

    def flip(at):
        cot_t_ref[:, at] = cot_ref[at, :].astype(f32).T.astype(bf16)

    lane_loop(length, flip)
    padded[...] = jnp.zeros_like(padded)
    for t in range(2):
        padded[t, skip:, :] = att_ref[t]
        copies[t].wait()
    mixed_ref[...] = (xt_ref[...].astype(f32) + dot(w_buf[0], padded[0], 1, 0)) + dot(w_buf[1], padded[1], 1, 0)

    def norm(at):
        v = mixed_ref[:, at]
        centred = v - jnp.mean(v, axis=0, keepdims=True)
        inverse = lax.rsqrt(jnp.mean(centred * centred, axis=0, keepdims=True) + ln_eps)
        normed_ref[:, at] = (centred * inverse * gain_ref[...] + shift_ref[...]).astype(bf16)

    lane_loop(length, norm)


def mlp_kernel(normed_ref, cot_ref, up_ref, down_ref, out_ref, grad_ref):
    @pl.when(pl.program_id(0) == 0)
    def _():
        out_ref[...] = jnp.zeros_like(out_ref)
        grad_ref[...] = jnp.zeros_like(grad_ref)

    width = up_ref.shape[1]
    start = 0
    while start < width:
        size = 512 if width - start >= 1024 else width - start
        up = up_ref[:, start : start + size]
        down = down_ref[:, start : start + size]
        hidden = dot(up, normed_ref[...], 0, 0)
        grad_active = dot(down, cot_ref[...], 0, 0)
        square = hidden * hidden
        half = 0.5 + 0.5 * jnp.tanh(hidden * (gelu_coeff + (gelu_coeff * 0.044715) * square))
        active = hidden * half
        slope = half + active * (1.0 - half) * (2.0 * gelu_coeff + (6.0 * 0.044715 * gelu_coeff) * square)
        out_ref[...] += dot(down, active.astype(bf16), 1, 0)
        grad_ref[...] += dot(up, (grad_active * slope).astype(bf16), 1, 0)
        start += size


def turn_kernel(skip, mixed_ref, out_ref, grad_ref, cot_ref, gain_ref, w_ref,
                output_ref, d_mixed_ref, d_att_ref, w_buf, sem):
    length = mixed_ref.shape[1]
    copies = []
    for t in range(2):
        copies.append(pltpu.make_async_copy(w_ref.at[t, :, pl.ds(w_ref.shape[2] - w_buf.shape[2], w_buf.shape[2])],
                                            w_buf.at[t], sem.at[t]))
        copies[t].start()

    def back(at):
        v = mixed_ref[:, at]
        output_ref[at, :] = (v + out_ref[:, at]).T.astype(bf16)
        centred = v - jnp.mean(v, axis=0, keepdims=True)
        inverse = lax.rsqrt(jnp.mean(centred * centred, axis=0, keepdims=True) + ln_eps)
        scaled = centred * inverse
        e = grad_ref[:, at] * gain_ref[...]
        d_norm = inverse * (e - jnp.mean(e, axis=0, keepdims=True)
                            - scaled * jnp.mean(e * scaled, axis=0, keepdims=True))
        d_mixed_ref[:, at] = cot_ref[:, at].astype(f32) + d_norm

    lane_loop(length, back)
    low = d_mixed_ref[...].astype(bf16)
    for t in range(2):
        copies[t].wait()
        d_att_ref[t] = dot(w_buf[t], low, 0, 0)[skip:].astype(bf16)


def finish_kernel(qkv_width, dqkv_ref, w_ref, normed_ref, inner_ref, downs_ref, ups_ref, xt_ref, d_mixed_ref, gain_ref,
                  patch_ref, up_grad_ref, down_grad_ref, total, through):
    length = xt_ref.shape[1]
    first = pl.program_id(0) == 0

    @pl.when(first)
    def _():
        total[...] = jnp.zeros_like(total)
        through[...] = jnp.zeros_like(through)

    total[...] += dot(w_ref[:, :qkv_width], dqkv_ref[...], 1, 0)
    through[...] += dot(ups_ref[...], dqkv_ref[...], 1, 0)
    up_grad_ref[...] = adapter_scale * dot(inner_ref[...], dqkv_ref[...], 1, 1)

    @pl.when(pl.program_id(0) == pl.num_programs(0) - 1)
    def _():
        low = (adapter_scale * through[...]).astype(bf16)
        down_grad_ref[...] = dot(low, normed_ref[...], 1, 1)
        total[...] += dot(downs_ref[...], low, 0, 0)

        def back(at):
            v = xt_ref[:, at].astype(f32)
            centred = v - jnp.mean(v, axis=0, keepdims=True)
            inverse = lax.rsqrt(jnp.mean(centred * centred, axis=0, keepdims=True) + ln_eps)
            scaled = centred * inverse
            e = total[:, at] * gain_ref[...]
            d_norm = inverse * (e - jnp.mean(e, axis=0, keepdims=True)
                                - scaled * jnp.mean(e * scaled, axis=0, keepdims=True))
            patch_ref[at, :] = (d_mixed_ref[:, at] + d_norm).T

        lane_loop(length, back)


def swap(values, use_low, swapped):
    half = values.shape[0] // 2
    window = jnp.where(use_low, values[:half], values[half:])
    other = lax.ppermute(window.astype(bf16), "tp", [(0, 1), (1, 0)])
    return jnp.where(swapped, jnp.concatenate([other, other]).astype(values.dtype), values)


def scatter_sum(value):
    def halve(value, axis_name, bit):
        size = lax.axis_size(axis_name)
        mine = (lax.axis_index(axis_name) // bit) % 2
        kept = lax.dynamic_index_in_dim(value, mine, 0, keepdims=False)
        sent = lax.dynamic_index_in_dim(value, 1 - mine, 0, keepdims=False)
        return kept + lax.ppermute(sent, axis_name, [(i, i ^ bit) for i in range(size)])

    rest = value.shape[1:]
    rows = lax.axis_size("rows")
    value = halve(value.reshape((2, rows) + rest), "tp", 1)
    bit = rows // 2
    while bit:
        value = halve(value.reshape((2, bit) + rest), "rows", bit)
        bit //= 2
    return value[0]


def shards(
    patches,
    image_lengths,
    ln_gain,
    ln_bias,
    query_key_value_weight,
    out_weight,
    up_weight,
    down_weight,
    adapter,
    adapter_mean,
    adapter_square,
    cotangent,
):
    tp_index = lax.axis_index("tp")
    both = ("tp", "rows")
    devices = lax.axis_size("tp") * lax.axis_size("rows")
    length, width = patches.shape[1:]
    depth, part = query_key_value_weight.shape[1:]
    heads = part // HD
    qkv_width = 3 * part
    square_width = 4 * part
    hidden_width = -(-up_weight.shape[1] // LANES) * LANES
    out_width = -(-part // LANES) * LANES
    skip = out_width - part
    own = adapter.shape[1] // RANK

    lengths = image_lengths[0]
    ends = jnp.cumsum(lengths, dtype=jnp.int32)
    start = jnp.sum(jnp.where(lengths == length, ends - lengths, 0))
    use_low = start <= length // 2
    place = lax.iota(jnp.int32, length)
    swapped = jnp.where(use_low, place < start, place >= start)
    position = place + length * jnp.where(swapped, 1 - tp_index, tp_index)
    segment = jnp.sum((position[:, None] >= ends[None, :]).astype(jnp.int32), axis=1)
    seg_col = jnp.broadcast_to(segment[:, None], (length, LANES))
    seg_row = segment[None, :]
    swapped = swapped[:, None]

    x = swap(patches[0], use_low, swapped)
    cot = swap(cotangent[0], use_low, swapped)

    if adapter.shape[1] % RANK == 0:
        local = adapter.astype(bf16).reshape(2, own, RANK).transpose(0, 2, 1)
        every = lax.all_gather(local, both, axis=0)
        every = every.transpose(1, 2, 0, 3).reshape(2, RANK, 3, width).transpose(0, 2, 1, 3)
    else:
        every = lax.all_gather(adapter.astype(bf16), both, axis=0).transpose(1, 0, 2)
        every = every.reshape(2, 3, width, RANK).transpose(0, 1, 3, 2)
    downs = every[0].reshape(3 * RANK, width)
    ups = every[1].reshape(3, RANK, 2, part).transpose(2, 0, 1, 3)
    ups = (ups[:, :, :, None, :] * jnp.eye(3, dtype=bf16)[None, :, None, :, None]).reshape(2, 3 * RANK, qkv_width)

    square = jnp.concatenate([query_key_value_weight[0], query_key_value_weight[1], query_key_value_weight[2], out_weight], axis=1)
    pad = ((0, 0), (0, hidden_width - up_weight.shape[1]))
    square = lax.all_gather(square, both, axis=0, tiled=True).reshape(2, width, square_width)
    up_all = lax.all_gather(jnp.pad(up_weight, pad), both, axis=0, tiled=True).reshape(2, width, hidden_width)
    down_all = lax.all_gather(jnp.pad(down_weight, pad), both, axis=0, tiled=True).reshape(2, width, hidden_width)

    column = lambda v: jnp.broadcast_to(v[:, None], (width, LANES))
    gain_one, gain_two = column(ln_gain[0]), column(ln_gain[1])
    shift_one, shift_two = column(ln_bias[0]), column(ln_bias[1])

    by_part = lambda rows, columns: pl.BlockSpec((None, rows, columns), lambda t: (t, 0, 0))
    qkv, x_t, normed_one, inner = call(
        functools.partial(project_kernel, qkv_width),
        (2,),
        [whole((length, width)), whole((width, LANES)), whole((width, LANES)), whole((3 * RANK, width)),
         by_part(3 * RANK, qkv_width), by_part(width, square_width)],
        [by_part(qkv_width, length), whole((width, length)), whole((width, length)), whole((3 * RANK, length))],
        [struct((2, qkv_width, length), bf16), struct((width, length), bf16), struct((width, length), bf16),
         struct((3 * RANK, length), bf16)],
    )(x, gain_one, shift_one, downs, ups, square)

    qkv = qkv.reshape(2, 3, heads, HD, length)
    head_of = lambda j: pl.BlockSpec((None, None, None, HD, length), lambda t, h: (t, j, h, 0, 0))
    head = pl.BlockSpec((None, None, HD, length), lambda t, h: (t, h, 0, 0))
    table = pl.BlockSpec((None, None, length, length), lambda t, h: (t, h, 0, 0))
    line = pl.BlockSpec((None, None, 1, length), lambda t, h: (t, h, 0, 0))
    attended, probs, inverse = call(
        attend_kernel,
        (2, heads),
        [head_of(0), head_of(1), head_of(2), whole((length, LANES)), whole((1, length))],
        [head, table, line],
        [struct((2, heads, HD, length), bf16), struct((2, heads, length, length), bf16),
         struct((2, heads, 1, length), f32)],
    )(qkv, qkv, qkv, seg_col, seg_row)

    hbm = pl.BlockSpec(memory_space=pl.ANY)
    mixed, normed_two, cot_t = call(
        functools.partial(mix_kernel, skip),
        (1,),
        [whole((width, length)), whole((2, part, length)), hbm, whole((width, LANES)), whole((width, LANES)),
         whole((length, width))],
        [whole((width, length))] * 3,
        [struct((width, length), f32), struct((width, length), bf16), struct((width, length), bf16)],
        [pltpu.VMEM((2, width, out_width), bf16), pltpu.VMEM((2, out_width, length), bf16), pltpu.SemaphoreType.DMA((2,))],
    )(x_t, attended.reshape(2, part, length), square, gain_two, shift_two, cot)

    fed, grad_two = call(
        mlp_kernel,
        (2,),
        [whole((width, length)), whole((width, length)), by_part(width, hidden_width), by_part(width, hidden_width)],
        [whole((width, length))] * 2,
        [struct((width, length), f32)] * 2,
    )(normed_two, cot_t, up_all, down_all)

    output, d_mixed, d_attended = call(
        functools.partial(turn_kernel, skip),
        (1,),
        [whole((width, length))] * 4 + [whole((width, LANES)), hbm],
        [whole((length, width)), whole((width, length)), whole((2, part, length))],
        [struct((length, width), bf16), struct((width, length), f32), struct((2, part, length), bf16)],
        [pltpu.VMEM((2, width, out_width), bf16), pltpu.SemaphoreType.DMA((2,))],
    )(mixed, fed, grad_two, cot_t, gain_two, square)

    three = pl.BlockSpec((None, 3, None, HD, length), lambda t, h: (t, 0, h, 0, 0))
    dqkv = call(
        attend_back_kernel,
        (2, heads),
        [table, line, head_of(0), head_of(1), head_of(2), head, head],
        three,
        struct((2, 3, heads, HD, length), bf16),
    )(probs, inverse, qkv, qkv, qkv, d_attended.reshape(2, heads, HD, length), attended)

    patch_grad, up_grad, down_grad = call(
        functools.partial(finish_kernel, qkv_width),
        (2,),
        [by_part(qkv_width, length), by_part(width, square_width), whole((width, length)), whole((3 * RANK, length)),
         whole((3 * RANK, width)), by_part(3 * RANK, qkv_width), whole((width, length)), whole((width, length)),
         whole((width, LANES))],
        [whole((length, width)), by_part(3 * RANK, qkv_width), whole((3 * RANK, width))],
        [struct((length, width), f32), struct((2, 3 * RANK, qkv_width), f32), struct((3 * RANK, width), f32)],
        [pltpu.VMEM((width, length), f32), pltpu.VMEM((3 * RANK, length), f32)],
    )(dqkv.reshape(2, qkv_width, length), square, normed_one, inner, downs, ups, x_t, d_mixed, gain_one)

    output = swap(output, use_low, swapped)
    patch_grad = swap(patch_grad, use_low, swapped)

    up_grad = up_grad.reshape(2, 3, RANK, 3, part)
    up_grad = jnp.stack([up_grad[:, j, :, j] for j in range(3)])
    grads = jnp.stack([
        down_grad.reshape(3, RANK, width).transpose(1, 0, 2).reshape(RANK, 3 * width),
        up_grad.transpose(2, 0, 1, 3).reshape(RANK, 3 * width),
    ])
    if adapter.shape[1] % RANK == 0:
        grads = grads.reshape(2, RANK, devices, own).transpose(2, 0, 1, 3)
        summed = scatter_sum(grads).transpose(0, 2, 1).reshape(2, own * RANK)
    else:
        grads = grads.transpose(0, 2, 1).reshape(2, devices, adapter.shape[1]).transpose(1, 0, 2)
        summed = scatter_sum(grads)

    adapter_grad = summed / math.sqrt(lax.axis_size("rows") * lax.axis_size("tp") * length)
    new_mean = beta_one * adapter_mean + (1.0 - beta_one) * adapter_grad
    new_square = beta_two * adapter_square + (1.0 - beta_two) * adapter_grad * adapter_grad
    fixed_mean = new_mean / (1.0 - beta_one**adam_step)
    fixed_square = new_square / (1.0 - beta_two**adam_step)
    new_adapter = adapter - learn_rate * (
        fixed_mean / (jnp.sqrt(fixed_square) + adam_eps) + decay_rate * adapter
    )
    return (output[None], patch_grad[None], adapter_grad, new_adapter, new_mean, new_square)


def solution(mesh):
    in_specs = (
        P("rows", "tp", None),
        P("rows", None),
        P(),
        P(),
        P(None, "rows", "tp"),
        P("rows", "tp"),
        P("rows", "tp"),
        P("rows", "tp"),
        P(None, ("tp", "rows")),
        P(None, ("tp", "rows")),
        P(None, ("tp", "rows")),
        P("rows", "tp", None),
    )
    out_specs = (
        P("rows", "tp", None),
        P("rows", "tp", None),
        P(None, ("tp", "rows")),
        P(None, ("tp", "rows")),
        P(None, ("tp", "rows")),
        P(None, ("tp", "rows")),
    )
    return jax.shard_map(shards, mesh=mesh, in_specs=in_specs, out_specs=out_specs, check_vma=False)
```
